128 devices in a mesh: row: 8 (over x, core), col: 16 (over y, z).
Axes of the slice: x: 4, y: 4, z: 4, core: 2. Of those that a mesh axis runs over, the one named last changes fastest.
Arguments:
- stiffness: bfloat16 [3584, 256, 256], P(('row', 'col')), may hold values from -0.25 to 0.25
- stiffness_index: int32 [3584, 2], P(('row', 'col')), may hold values from 0 to 15
- mode_basis: bfloat16 [524288, 256], P(('row', 'col')), may hold values from -0.75 to 0.75
- pair_owner: int32 [128, 2], replicated, may hold values from 0 to 1
- margin: int32 [128, 2, 4, 2], replicated, may hold values from 0 to 15
Outputs:
- coarse: bfloat16 [128, 128, 256, 256], P('row', None, 'col')
The draws below stay inside these ranges and needn't reach their ends.
All inputs are finite; a program needn't handle non-finite values.
Results may differ from the reference program's by a relative error of at most 0.0049.
Values may be sent and summed in bfloat16 or wider, within the bound.
No kernel may reach another device: no remote copies, remote signals or barrier semaphores. Data moves between devices by JAX's collectives and lax.ppermute only.
A program may use at most 128 MiB of HBM per device.

```python
import jax
import jax.numpy as jnp
import numpy as np
from jax import lax

M = 256
BS = 256
NB = 16
NK = 28
OVB = 4
NLOC = 4096
S = 128
N_ROW = 8
N_COL = 16


def with_ends(array, own_key, smallest, top_value):
    spot = [jax.random.randint(jax.random.fold_in(own_key, axis), (), 0, length) for axis, length in enumerate(array.shape)]
    longest = array.shape.index(max(array.shape))
    beside = spot[:longest] + [(spot[longest] + 1) % array.shape[longest]] + spot[longest + 1:]
    return array.at[tuple(spot)].set(smallest).at[tuple(beside)].set(top_value)


def block_scale(rng, dims, split, low, high):
    gain = 1.0
    for dim, blocks in split:
        steps = jax.random.uniform(jax.random.fold_in(jax.random.fold_in(rng, 6), dim), (blocks,), jnp.float32, low / len(split), high / len(split))
        gain = gain * jnp.repeat(jnp.exp(steps), dims[dim] // blocks).reshape((-1,) + (1,) * (len(dims) - 1 - dim))
    return gain


def centred(stream_key, dims, deviation, reach, shards=(), kind=jnp.bfloat16):
    values = deviation * jax.random.normal(stream_key, dims, jnp.float32)
    if shards:
        values = values * block_scale(stream_key, dims, shards, -0.22, 0.18)
    return jnp.clip(values, -reach, reach).astype(kind)


def setup_inputs(seed: int = 0) -> dict:
    keys = jax.random.split(jax.random.key(seed), 6)
    return {
        "stiffness": centred(keys[0], (S * NK, BS, BS), (2 * BS) ** -0.5, 0.25, ((0, 128),)),
        "stiffness_index": with_ends(jax.random.randint(keys[1], (S * NK, 2), 0, NB), jax.random.fold_in(keys[1], 1), 0, NB - 1).astype(jnp.int32),
        "mode_basis": centred(keys[2], (S * NLOC, M), 0.125, 0.75, ((0, 128),)),
        "pair_owner": with_ends(jax.random.randint(keys[3], (S, 2), 0, 2), jax.random.fold_in(keys[3], 1), 0, 1).astype(jnp.int32),
        "margin": with_ends(jax.random.randint(keys[4], (S, 2, OVB, 2), 0, NB), jax.random.fold_in(keys[4], 1), 0, NB - 1).astype(jnp.int32),
    }


def reference(stiffness, stiffness_index, mode_basis, pair_owner, margin):
    blocks_all = stiffness.reshape(S, NK, BS, BS)
    index_all = stiffness_index.reshape(S, NK, 2)
    modes_all = mode_basis.reshape(S, NB, BS, M)

    def local_apply(inputs):
        stiff_blocks, indices, mode_blocks = inputs
        picked = mode_blocks[indices[:, 1]]
        products = jnp.einsum('kab,kbm->kam', stiff_blocks.astype(jnp.float32), picked.astype(jnp.float32),
                              precision=lax.Precision.HIGHEST)
        selector = (indices[:, 0][None, :] == jnp.arange(NB, dtype=jnp.int32)[:, None]).astype(jnp.float32)
        summed = jnp.einsum('nk,kam->nam', selector, products, precision=lax.Precision.HIGHEST)
        applied = summed.astype(jnp.bfloat16)
        diagonal = jnp.dot(mode_blocks.reshape(NLOC, M).T, applied.reshape(NLOC, M),
                           preferred_element_type=jnp.float32).astype(jnp.bfloat16)
        return applied, diagonal

    applied_all, diagonals = lax.map(local_apply, (blocks_all, index_all, modes_all))

    def project_pair(inputs):
        first, second, direction = inputs
        owner_flag = pair_owner[first, direction]
        lists = margin[first, direction]
        own_modes = modes_all[first][lists[:, 0]]
        own_applied = applied_all[first][lists[:, 0]]
        far_modes = modes_all[second][lists[:, 1]]
        far_applied = applied_all[second][lists[:, 1]]
        left = jnp.where(owner_flag == 0, own_modes, own_applied).reshape(OVB * BS, M)
        right = jnp.where(owner_flag == 0, far_applied, far_modes).reshape(OVB * BS, M)
        return jnp.dot(left.T, right, preferred_element_type=jnp.float32).astype(jnp.bfloat16)

    numbers = np.arange(S, dtype=np.int32)
    group_of = numbers // N_COL
    place_of = numbers % N_COL
    col_first = numbers[place_of < N_COL - 1]
    row_first = numbers[group_of < N_ROW - 1]
    firsts = np.concatenate([col_first, row_first]).astype(np.int32)
    seconds = np.concatenate([col_first + 1, row_first + N_COL]).astype(np.int32)
    directions = np.concatenate([np.zeros(col_first.shape[0], np.int32), np.ones(row_first.shape[0], np.int32)])
    pair_blocks = lax.map(project_pair, (jnp.asarray(firsts), jnp.asarray(seconds), jnp.asarray(directions)))

    result = jnp.zeros((S, S, M, M), jnp.bfloat16)
    result = result.at[numbers, numbers].set(diagonals)
    result = result.at[firsts, seconds].set(pair_blocks)
    return result
```

```python
import functools

import jax
import jax.numpy as jnp
from jax import lax
from jax.experimental import pallas as pl
from jax.experimental.pallas import tpu as pltpu
from jax.sharding import PartitionSpec as P

F32 = jnp.float32
BF16 = jnp.bfloat16
ANY = pl.BlockSpec(memory_space=pl.ANY)
VMEM = pl.BlockSpec(memory_space=pltpu.VMEM)
SMEM = pl.BlockSpec(memory_space=pltpu.SMEM)


def place():
    row = lax.axis_index("row")
    col = lax.axis_index("col")
    sub = row * lax.axis_size("col") + col
    return row, col, sub, lax.rem(row, 2)


def side_block(owners, lists, direction, first, side, j):
    use_applied = owners[direction, first] + side == 1
    return lists[direction, j, side, first], use_applied


def sides(sub, odd, cols):
    before = jnp.maximum(sub - 1, 0)
    above = jnp.maximum(sub - cols, 0)
    send_col = (0, jnp.where(odd == 1, sub, before), 1 - odd)
    send_row = (1, above, 1)
    keep_col = (0, jnp.where(odd == 1, before, sub), odd)
    keep_row = (1, sub, 0)
    return send_col, send_row, keep_col, keep_row


def apply_kernel(
    nk, cols, index_hbm, owner_hbm, margin_hbm, stiff_hbm, modes_hbm,
    applied_ref, send_col_ref, send_row_ref,
    index, owners, lists, stiff, modes, total, small_sem, mode_sem, stiff_sem,
):
    small = [
        pltpu.make_async_copy(src, dst, small_sem.at[i])
        for i, (src, dst) in enumerate(((index_hbm, index), (owner_hbm, owners), (margin_hbm, lists)))
    ]
    mode_copy = pltpu.make_async_copy(modes_hbm, modes, mode_sem)
    stiff_copies = [
        pltpu.make_async_copy(stiff_hbm.at[k], stiff.at[k], stiff_sem.at[k]) for k in range(nk)
    ]
    small[0].start()
    mode_copy.start()
    for k in range(nk):
        stiff_copies[k].start()
    small[1].start()
    small[2].start()
    total[...] = jnp.zeros_like(total)
    small[0].wait()
    mode_copy.wait()
    for k in range(nk):
        stiff_copies[k].wait()
        product = jnp.dot(stiff[k], modes[index[1, k]], preferred_element_type=F32)
        a = index[0, k]
        total[a] = total[a] + product
    for a in range(applied_ref.shape[0]):
        applied_ref[a] = total[a].astype(BF16)
    small[1].wait()
    small[2].wait()
    _, _, sub, odd = place()
    send_col, send_row, _, _ = sides(sub, odd, cols)
    for out, (direction, first, side) in ((send_col_ref, send_col), (send_row_ref, send_row)):
        for j in range(out.shape[0]):
            block, use_applied = side_block(owners, lists, direction, first, side, j)

            @pl.when(use_applied)
            def _():
                out[j] = applied_ref[block]

            @pl.when(jnp.logical_not(use_applied))
            def _():
                out[j] = modes[block]


def middle_kernel(
    cols, owners, lists, modes, applied, stored, diag_ref, keep_col_ref, keep_row_ref,
    zeros, total, zero_sem,
):
    zeros[...] = jnp.zeros_like(zeros)
    fills = [
        pltpu.make_async_copy(zeros, stored.at[i], zero_sem.at[i]) for i in range(stored.shape[0])
    ]
    for fill in fills:
        fill.start()
    _, _, sub, odd = place()
    _, _, keep_col, keep_row = sides(sub, odd, cols)
    bs = modes.shape[1]
    for out, (direction, first, side) in ((keep_col_ref, keep_col), (keep_row_ref, keep_row)):
        for j in range(out.shape[1] // bs):
            block, use_applied = side_block(owners, lists, direction, first, side, j)

            @pl.when(use_applied)
            def _():
                out[:, j * bs : (j + 1) * bs] = applied[block].T

            @pl.when(jnp.logical_not(use_applied))
            def _():
                out[:, j * bs : (j + 1) * bs] = modes[block].T

    total[...] = jnp.zeros_like(total)

    def step(a, carry):
        total[...] += lax.dot_general(
            modes[a], applied[a], (((0,), (0,)), ((), ())), preferred_element_type=F32
        )
        return carry

    lax.fori_loop(0, modes.shape[0], step, 0)
    diag_ref[...] = total[...].astype(BF16)
    for fill in fills:
        fill.wait()


def project_kernel(diag, keep_col, keep_row, got_col, got_row, pieces):
    part = pieces.shape[1] // 3
    row_block = jnp.dot(keep_row[...], got_row[...], preferred_element_type=F32).astype(BF16)
    col_block = jnp.dot(keep_col[...], got_col[...], preferred_element_type=F32)
    odd = lax.rem(lax.axis_index("row"), 2)
    for c in range(pieces.shape[0]):
        pieces[c, 0:part] = diag[c * part : (c + 1) * part]
        pieces[c, 2 * part : 3 * part] = row_block[c * part : (c + 1) * part]

    def spread(block):
        for c in range(pieces.shape[0]):
            pieces[c, part : 2 * part] = block[c * part : (c + 1) * part]

    @pl.when(odd == 0)
    def _():
        spread(col_block.astype(BF16))

    @pl.when(odd == 1)
    def _():
        spread(col_block.T.astype(BF16))


def store_kernel(rows, received, zeroed, stored, sems):
    del zeroed
    cols = received.shape[0]
    part = received.shape[1] // 3
    row = lax.axis_index("row")
    odd = lax.rem(row, 2)
    base = row * cols

    def copies(act):
        for c in range(cols):
            act(pltpu.make_async_copy(received.at[c, 0:part], stored.at[c, base + c], sems.at[0, c]))

            def col_copy(local):
                act(
                    pltpu.make_async_copy(
                        received.at[c, part : 2 * part], stored.at[local, base + local + 1], sems.at[1, c]
                    )
                )

            if c < cols - 1:
                pl.when(odd == 0)(functools.partial(col_copy, c))
            if c > 0:
                pl.when(odd == 1)(functools.partial(col_copy, c - 1))

        @pl.when(row < rows - 1)
        def _():
            for c in range(cols):
                act(
                    pltpu.make_async_copy(
                        received.at[c, 2 * part : 3 * part], stored.at[c, base + cols + c], sems.at[2, c]
                    )
                )

    copies(lambda copy: copy.start())
    copies(lambda copy: copy.wait())


def params(mib):
    return pltpu.CompilerParams(vmem_limit_bytes=mib << 20)


def on_device(stiffness, stiffness_index, mode_basis, pair_owner, margin):
    rows = lax.axis_size("row")
    cols = lax.axis_size("col")
    nk, bs, _ = stiffness.shape
    m = mode_basis.shape[1]
    nb = mode_basis.shape[0] // bs
    ovb = margin.shape[2]
    modes = mode_basis.reshape(nb, bs, m)
    index = stiffness_index.T
    owners = pair_owner.T
    lists = margin.transpose(1, 2, 3, 0)
    shape = jax.ShapeDtypeStruct
    applied, send_col, send_row = pl.pallas_call(
        functools.partial(apply_kernel, nk, cols),
        out_shape=(shape((nb, bs, m), BF16), shape((ovb, bs, m), BF16), shape((ovb, bs, m), BF16)),
        in_specs=[ANY] * 5,
        out_specs=(VMEM, VMEM, VMEM),
        scratch_shapes=[
            pltpu.SMEM(index.shape, jnp.int32),
            pltpu.SMEM(owners.shape, jnp.int32),
            pltpu.SMEM(lists.shape, jnp.int32),
            pltpu.VMEM((nk, bs, bs), BF16),
            pltpu.VMEM((nb, bs, m), BF16),
            pltpu.VMEM((nb, bs, m), F32),
            pltpu.SemaphoreType.DMA((3,)),
            pltpu.SemaphoreType.DMA,
            pltpu.SemaphoreType.DMA((nk,)),
        ],
        compiler_params=params(20),
        cost_estimate=pl.CostEstimate(
            flops=2 * nk * bs * bs * m, bytes_accessed=2 * (stiffness.size + 2 * mode_basis.size), transcendentals=0
        ),
        name="apply",
    )(index, owners, lists, stiffness, modes)

    flat = rows * cols
    line = [(d, d - 1) for d in range(flat) if (d // cols) % 2 == 0 and d % cols > 0]
    line += [(d, d + 1) for d in range(flat) if (d // cols) % 2 == 1 and d % cols < cols - 1]
    got_col = lax.ppermute(send_col, ("row", "col"), line)
    got_row = lax.ppermute(send_row, "row", [(r, r - 1) for r in range(1, rows)])

    total = rows * cols
    part = m // cols
    stored, diag, keep_col, keep_row = pl.pallas_call(
        functools.partial(middle_kernel, cols),
        out_shape=(
            shape((cols, total, part, m), BF16),
            shape((m, m), BF16),
            shape((m, ovb * bs), BF16),
            shape((m, ovb * bs), BF16),
        ),
        in_specs=[SMEM, SMEM, VMEM, VMEM],
        out_specs=(ANY, VMEM, VMEM, VMEM),
        scratch_shapes=[
            pltpu.VMEM((total, part, m), BF16),
            pltpu.VMEM((m, m), F32),
            pltpu.SemaphoreType.DMA((cols,)),
        ],
        compiler_params=params(12),
        cost_estimate=pl.CostEstimate(
            flops=2 * mode_basis.size * m, bytes_accessed=2 * cols * total * part * m, transcendentals=0
        ),
        name="middle",
    )(owners, lists, modes, applied)

    pieces = pl.pallas_call(
        project_kernel,
        out_shape=shape((cols, 3 * part, m), BF16),
        in_specs=[VMEM] * 5,
        out_specs=VMEM,
        compiler_params=params(12),
        cost_estimate=pl.CostEstimate(
            flops=4 * ovb * bs * m * m, bytes_accessed=8 * ovb * bs * m, transcendentals=0
        ),
        name="project",
    )(diag, keep_col, keep_row, got_col.reshape(ovb * bs, m), got_row.reshape(ovb * bs, m))

    received = lax.all_to_all(pieces, "col", split_axis=0, concat_axis=0, tiled=True)

    return pl.pallas_call(
        functools.partial(store_kernel, rows),
        out_shape=shape(stored.shape, BF16),
        in_specs=[VMEM, ANY],
        out_specs=ANY,
        scratch_shapes=[pltpu.SemaphoreType.DMA((3, cols))],
        input_output_aliases={1: 0},
        compiler_params=params(12),
        name="store",
    )(received, stored)


def solution(mesh):
    return jax.shard_map(
        on_device,
        mesh=mesh,
        in_specs=(
            P(("row", "col"), None, None),
            P(("row", "col"), None),
            P(("row", "col"), None),
            P(),
            P(),
        ),
        out_specs=P("row", None, "col", None),
        check_vma=False,
    )
```

```python
import functools

import jax
import jax.numpy as jnp
from jax import lax
from jax.experimental import pallas as pl
from jax.experimental.pallas import tpu as pltpu
from jax.sharding import PartitionSpec as P

F32 = jnp.float32
BF16 = jnp.bfloat16
HBM = pl.BlockSpec(memory_space=pltpu.HBM)
VMEM = pl.BlockSpec(memory_space=pltpu.VMEM)


def place():
    row = lax.axis_index("row")
    col = lax.axis_index("col")
    sub = row * lax.axis_size("col") + col
    return row, col, sub, lax.rem(row, 2)


def side_block(owners, lists, direction, first, side, j):
    use_applied = owners[direction, first] + side == 1
    return lists[direction, j, side, first], use_applied


def sides(sub, odd, cols):
    before = jnp.maximum(sub - 1, 0)
    above = jnp.maximum(sub - cols, 0)
    send_col = (0, jnp.where(odd == 1, sub, before), 1 - odd)
    send_row = (1, above, 1)
    keep_col = (0, jnp.where(odd == 1, before, sub), odd)
    keep_row = (1, sub, 0)
    return send_col, send_row, keep_col, keep_row


def apply_kernel(
    nk, cols, groups, index_hbm, owner_hbm, margin_hbm, stiff_hbm, modes_hbm,
    total, modes, send_col_ref, send_row_ref,
    index, owners, lists, stiff, small_sem, mode_sem, stiff_sem,
):
    small = [
        pltpu.make_async_copy(src, dst, small_sem.at[i])
        for i, (src, dst) in enumerate(((index_hbm, index), (owner_hbm, owners), (margin_hbm, lists)))
    ]
    mode_copy = pltpu.make_async_copy(modes_hbm, modes, mode_sem)
    edges = [nk * g // groups for g in range(groups + 1)]
    stiff_copies = [
        pltpu.make_async_copy(
            stiff_hbm.at[pl.ds(lo, hi - lo)], stiff.at[pl.ds(lo, hi - lo)], stiff_sem.at[g]
        )
        for g, (lo, hi) in enumerate(zip(edges, edges[1:]))
    ]
    small[0].start()
    mode_copy.start()
    for copy in stiff_copies:
        copy.start()
    small[1].start()
    small[2].start()
    total[...] = jnp.zeros_like(total)
    for copy in small:
        copy.wait()
    mode_copy.wait()
    for g in range(groups):
        stiff_copies[g].wait()
        for k in range(edges[g], edges[g + 1]):
            product = jnp.dot(stiff[k], modes[index[1, k]], preferred_element_type=F32)
            a = index[0, k]
            total[a] = total[a] + product
    _, _, sub, odd = place()
    send_col, send_row, _, _ = sides(sub, odd, cols)
    for out, (direction, first, side) in ((send_row_ref, send_row), (send_col_ref, send_col)):
        for j in range(out.shape[0]):
            block, use_applied = side_block(owners, lists, direction, first, side, j)

            @pl.when(use_applied)
            def _():
                out[j] = total[block].astype(BF16)

            @pl.when(jnp.logical_not(use_applied))
            def _():
                out[j] = modes[block]


def middle_kernel(
    cols, owner_hbm, margin_hbm, modes, applied, stored, diag_ref, keep_col_ref, keep_row_ref,
    owners, lists, zeros, total, small_sem, zero_sem,
):
    small = [
        pltpu.make_async_copy(src, dst, small_sem.at[i])
        for i, (src, dst) in enumerate(((owner_hbm, owners), (margin_hbm, lists)))
    ]
    for copy in small:
        copy.start()
    zeros[...] = jnp.zeros_like(zeros)
    fills = [
        pltpu.make_async_copy(zeros, stored.at[i], zero_sem.at[i]) for i in range(stored.shape[0])
    ]
    for fill in fills:
        fill.start()
    total[...] = jnp.zeros_like(total)

    def step(a, carry):
        total[...] += lax.dot_general(
            modes[a], applied[a].astype(BF16), (((0,), (0,)), ((), ())), preferred_element_type=F32
        )
        return carry

    lax.fori_loop(0, modes.shape[0], step, 0)
    diag_ref[...] = total[...].astype(BF16)
    for copy in small:
        copy.wait()
    _, _, sub, odd = place()
    _, _, keep_col, keep_row = sides(sub, odd, cols)
    bs = modes.shape[1]
    for out, (direction, first, side) in ((keep_col_ref, keep_col), (keep_row_ref, keep_row)):
        for j in range(out.shape[1] // bs):
            block, use_applied = side_block(owners, lists, direction, first, side, j)

            @pl.when(use_applied)
            def _():
                out[:, j * bs : (j + 1) * bs] = applied[block].astype(BF16).T

            @pl.when(jnp.logical_not(use_applied))
            def _():
                out[:, j * bs : (j + 1) * bs] = modes[block].T

    for fill in fills:
        fill.wait()


def project_kernel(diag, keep_col, keep_row, got_col, got_row, pieces):
    part = pieces.shape[1] // 3
    row_block = jnp.dot(keep_row[...], got_row[...], preferred_element_type=F32).astype(BF16)
    col_block = jnp.dot(keep_col[...], got_col[...], preferred_element_type=F32)
    odd = lax.rem(lax.axis_index("row"), 2)
    for c in range(pieces.shape[0]):
        pieces[c, 0:part] = diag[c * part : (c + 1) * part]
        pieces[c, 2 * part : 3 * part] = row_block[c * part : (c + 1) * part]

    def spread(block):
        for c in range(pieces.shape[0]):
            pieces[c, part : 2 * part] = block[c * part : (c + 1) * part]

    @pl.when(odd == 0)
    def _():
        spread(col_block.astype(BF16))

    @pl.when(odd == 1)
    def _():
        spread(col_block.T.astype(BF16))


def store_kernel(rows, received, zeroed, stored, sems):
    del zeroed
    cols = received.shape[0]
    part = received.shape[1] // 3
    row = lax.axis_index("row")
    odd = lax.rem(row, 2)
    base = row * cols

    def copies(act):
        for c in range(cols):
            act(pltpu.make_async_copy(received.at[c, 0:part], stored.at[c, base + c], sems.at[0, c]))

            def col_copy(local):
                act(
                    pltpu.make_async_copy(
                        received.at[c, part : 2 * part], stored.at[local, base + local + 1], sems.at[1, c]
                    )
                )

            if c < cols - 1:
                pl.when(odd == 0)(functools.partial(col_copy, c))
            if c > 0:
                pl.when(odd == 1)(functools.partial(col_copy, c - 1))

        @pl.when(row < rows - 1)
        def _():
            for c in range(cols):
                act(
                    pltpu.make_async_copy(
                        received.at[c, 2 * part : 3 * part], stored.at[c, base + cols + c], sems.at[2, c]
                    )
                )

    copies(lambda copy: copy.start())
    copies(lambda copy: copy.wait())


def params(mib):
    return pltpu.CompilerParams(vmem_limit_bytes=mib << 20)


def on_device(stiffness, stiffness_index, mode_basis, pair_owner, margin):
    rows = lax.axis_size("row")
    cols = lax.axis_size("col")
    nk, bs, _ = stiffness.shape
    m = mode_basis.shape[1]
    nb = mode_basis.shape[0] // bs
    ovb = margin.shape[2]
    modes = mode_basis.reshape(nb, bs, m)
    index = stiffness_index.T
    owners = pair_owner.T
    lists = margin.transpose(1, 2, 3, 0)
    groups = 2
    hbm = lambda x: pltpu.with_memory_space_constraint(x, pltpu.HBM)
    total, modes_near, send_col, send_row = pl.pallas_call(
        functools.partial(apply_kernel, nk, cols, groups),
        out_shape=(
            pltpu.VMEM((nb, bs, m), F32),
            pltpu.VMEM((nb, bs, m), BF16),
            pltpu.VMEM((ovb, bs, m), BF16),
            pltpu.VMEM((ovb, bs, m), BF16),
        ),
        in_specs=[HBM] * 5,
        out_specs=(VMEM,) * 4,
        scratch_shapes=[
            pltpu.SMEM(index.shape, jnp.int32),
            pltpu.SMEM(owners.shape, jnp.int32),
            pltpu.SMEM(lists.shape, jnp.int32),
            pltpu.VMEM((nk, bs, bs), BF16),
            pltpu.SemaphoreType.DMA((3,)),
            pltpu.SemaphoreType.DMA,
            pltpu.SemaphoreType.DMA((groups,)),
        ],
        compiler_params=params(20),
        cost_estimate=pl.CostEstimate(
            flops=2 * nk * bs * bs * m, bytes_accessed=2 * (stiffness.size + 2 * mode_basis.size), transcendentals=0
        ),
        name="apply",
    )(hbm(index), hbm(owners), hbm(lists), hbm(stiffness), hbm(modes))

    got_row = lax.ppermute(send_row, "row", [(r, r - 1) for r in range(1, rows)])
    flat = rows * cols
    line = [(d, d - 1) for d in range(flat) if (d // cols) % 2 == 0 and d % cols > 0]
    line += [(d, d + 1) for d in range(flat) if (d // cols) % 2 == 1 and d % cols < cols - 1]
    got_col = lax.ppermute(send_col, ("row", "col"), line)

    part = m // cols
    stored, diag, keep_col, keep_row = pl.pallas_call(
        functools.partial(middle_kernel, cols),
        out_shape=(
            pltpu.HBM((cols, flat, part, m), BF16),
            pltpu.VMEM((m, m), BF16),
            pltpu.VMEM((m, ovb * bs), BF16),
            pltpu.VMEM((m, ovb * bs), BF16),
        ),
        in_specs=[HBM, HBM, VMEM, VMEM],
        out_specs=(HBM, VMEM, VMEM, VMEM),
        scratch_shapes=[
            pltpu.SMEM(owners.shape, jnp.int32),
            pltpu.SMEM(lists.shape, jnp.int32),
            pltpu.VMEM((flat, part, m), BF16),
            pltpu.VMEM((m, m), F32),
            pltpu.SemaphoreType.DMA((2,)),
            pltpu.SemaphoreType.DMA((cols,)),
        ],
        compiler_params=params(12),
        cost_estimate=pl.CostEstimate(
            flops=2 * mode_basis.size * m, bytes_accessed=2 * cols * flat * part * m, transcendentals=0
        ),
        name="middle",
    )(hbm(owners), hbm(lists), modes_near, total)

    pieces = pl.pallas_call(
        project_kernel,
        out_shape=pltpu.VMEM((cols, 3 * part, m), BF16),
        in_specs=[VMEM] * 5,
        out_specs=VMEM,
        compiler_params=params(12),
        cost_estimate=pl.CostEstimate(
            flops=4 * ovb * bs * m * m, bytes_accessed=8 * ovb * bs * m, transcendentals=0
        ),
        name="project",
    )(diag, keep_col, keep_row, got_col.reshape(ovb * bs, m), got_row.reshape(ovb * bs, m))

    received = lax.all_to_all(pieces, "col", split_axis=0, concat_axis=0, tiled=True)

    return pl.pallas_call(
        functools.partial(store_kernel, rows),
        out_shape=pltpu.HBM(stored.shape, BF16),
        in_specs=[VMEM, HBM],
        out_specs=HBM,
        scratch_shapes=[pltpu.SemaphoreType.DMA((3, cols))],
        input_output_aliases={1: 0},
        compiler_params=params(12),
        name="store",
    )(received, stored)


def solution(mesh):
    return jax.shard_map(
        on_device,
        mesh=mesh,
        in_specs=(
            P(("row", "col"), None, None),
            P(("row", "col"), None),
            P(("row", "col"), None),
            P(),
            P(),
        ),
        out_specs=P("row", None, "col", None),
        check_vma=False,
    )
```

```python
import functools

import jax
import jax.numpy as jnp
from jax import lax
from jax.experimental import pallas as pl
from jax.experimental.pallas import tpu as pltpu
from jax.sharding import PartitionSpec as P

F32 = jnp.float32
BF16 = jnp.bfloat16
HBM = pl.BlockSpec(memory_space=pltpu.HBM)
VMEM = pl.BlockSpec(memory_space=pltpu.VMEM)


def place():
    row = lax.axis_index("row")
    col = lax.axis_index("col")
    sub = row * lax.axis_size("col") + col
    return row, col, sub, lax.rem(row, 2)


def exchange_order(cols):
    side = int(cols**0.5)
    y0, z0 = side // 2, side // 2
    return [(y0 + i + j) % side * side + (z0 + j) % side for i in range(side) for j in range(side)]


def side_block(owners, lists, direction, first, side, j):
    use_applied = owners[direction, first] + side == 1
    return lists[direction, j, side, first], use_applied


def sides(sub, odd, cols):
    before = jnp.maximum(sub - 1, 0)
    above = jnp.maximum(sub - cols, 0)
    send_col = (0, jnp.where(odd == 1, sub, before), 1 - odd)
    send_row = (1, above, 1)
    keep_col = (0, jnp.where(odd == 1, before, sub), odd)
    keep_row = (1, sub, 0)
    return send_col, send_row, keep_col, keep_row


def apply_kernel(
    nk, cols, groups, index_hbm, owner_hbm, margin_hbm, stiff_hbm, modes_hbm,
    total, modes, send_col_ref, send_row_ref,
    index, owners, lists, stiff, small_sem, mode_sem, stiff_sem,
):
    small = [
        pltpu.make_async_copy(src, dst, small_sem.at[i])
        for i, (src, dst) in enumerate(((index_hbm, index), (owner_hbm, owners), (margin_hbm, lists)))
    ]
    mode_copy = pltpu.make_async_copy(modes_hbm, modes, mode_sem)
    edges = [nk * g // groups for g in range(groups + 1)]
    stiff_copies = [
        pltpu.make_async_copy(
            stiff_hbm.at[pl.ds(lo, hi - lo)], stiff.at[pl.ds(lo, hi - lo)], stiff_sem.at[g]
        )
        for g, (lo, hi) in enumerate(zip(edges, edges[1:]))
    ]
    small[0].start()
    mode_copy.start()
    for copy in stiff_copies:
        copy.start()
    small[1].start()
    small[2].start()
    total[...] = jnp.zeros_like(total)
    for copy in small:
        copy.wait()
    mode_copy.wait()
    for g in range(groups):
        stiff_copies[g].wait()
        for k in range(edges[g], edges[g + 1]):
            product = jnp.dot(stiff[k], modes[index[1, k]], preferred_element_type=F32)
            a = index[0, k]
            total[a] = total[a] + product
    _, _, sub, odd = place()
    send_col, send_row, _, _ = sides(sub, odd, cols)
    for out, (direction, first, side) in ((send_row_ref, send_row), (send_col_ref, send_col)):
        for j in range(out.shape[0]):
            block, use_applied = side_block(owners, lists, direction, first, side, j)

            @pl.when(use_applied)
            def _():
                out[j] = total[block].astype(BF16)

            @pl.when(jnp.logical_not(use_applied))
            def _():
                out[j] = modes[block]


def middle_kernel(
    cols, owner_hbm, margin_hbm, modes, applied, stored, diag_ref, keep_col_ref, keep_row_ref,
    owners, lists, zeros, total, small_sem, zero_sem,
):
    small = [
        pltpu.make_async_copy(src, dst, small_sem.at[i])
        for i, (src, dst) in enumerate(((owner_hbm, owners), (margin_hbm, lists)))
    ]
    for copy in small:
        copy.start()
    zeros[...] = jnp.zeros_like(zeros)
    fills = [
        pltpu.make_async_copy(zeros, stored.at[i], zero_sem.at[i]) for i in range(stored.shape[0])
    ]
    for fill in fills:
        fill.start()
    total[...] = jnp.zeros_like(total)

    def step(a, carry):
        total[...] += lax.dot_general(
            modes[a], applied[a].astype(BF16), (((0,), (0,)), ((), ())), preferred_element_type=F32
        )
        return carry

    lax.fori_loop(0, modes.shape[0], step, 0)
    diag_ref[...] = total[...].astype(BF16)
    for copy in small:
        copy.wait()
    _, _, sub, odd = place()
    _, _, keep_col, keep_row = sides(sub, odd, cols)
    bs = modes.shape[1]
    for out, (direction, first, side) in ((keep_col_ref, keep_col), (keep_row_ref, keep_row)):
        for j in range(out.shape[1] // bs):
            block, use_applied = side_block(owners, lists, direction, first, side, j)

            @pl.when(use_applied)
            def _():
                out[:, j * bs : (j + 1) * bs] = applied[block].astype(BF16).T

            @pl.when(jnp.logical_not(use_applied))
            def _():
                out[:, j * bs : (j + 1) * bs] = modes[block].T

    for fill in fills:
        fill.wait()


def project_kernel(order, diag, keep_col, keep_row, got_col, got_row, pieces):
    part = pieces.shape[1] // 3
    row_block = jnp.dot(keep_row[...], got_row[...], preferred_element_type=F32).astype(BF16)
    col_block = jnp.dot(keep_col[...], got_col[...], preferred_element_type=F32)
    odd = lax.rem(lax.axis_index("row"), 2)
    for p, c in enumerate(order):
        pieces[p, 0:part] = diag[c * part : (c + 1) * part]
        pieces[p, 2 * part : 3 * part] = row_block[c * part : (c + 1) * part]

    def spread(block):
        for p, c in enumerate(order):
            pieces[p, part : 2 * part] = block[c * part : (c + 1) * part]

    @pl.when(odd == 0)
    def _():
        spread(col_block.astype(BF16))

    @pl.when(odd == 1)
    def _():
        spread(col_block.T.astype(BF16))


def store_kernel(rows, order, received, zeroed, stored, sems):
    del zeroed
    cols = received.shape[0]
    part = received.shape[1] // 3
    row = lax.axis_index("row")
    odd = lax.rem(row, 2)
    base = row * cols

    def copies(act):
        for p, c in enumerate(order):
            act(pltpu.make_async_copy(received.at[p, 0:part], stored.at[c, base + c], sems.at[0, c]))

            def col_copy(p, local):
                act(
                    pltpu.make_async_copy(
                        received.at[p, part : 2 * part], stored.at[local, base + local + 1], sems.at[1, p]
                    )
                )

            if c < cols - 1:
                pl.when(odd == 0)(functools.partial(col_copy, p, c))
            if c > 0:
                pl.when(odd == 1)(functools.partial(col_copy, p, c - 1))

        @pl.when(row < rows - 1)
        def _():
            for p, c in enumerate(order):
                act(
                    pltpu.make_async_copy(
                        received.at[p, 2 * part : 3 * part], stored.at[c, base + cols + c], sems.at[2, c]
                    )
                )

    copies(lambda copy: copy.start())
    copies(lambda copy: copy.wait())


def params(mib):
    return pltpu.CompilerParams(vmem_limit_bytes=mib << 20)


def on_device(stiffness, stiffness_index, mode_basis, pair_owner, margin):
    rows = lax.axis_size("row")
    cols = lax.axis_size("col")
    nk, bs, _ = stiffness.shape
    m = mode_basis.shape[1]
    nb = mode_basis.shape[0] // bs
    ovb = margin.shape[2]
    modes = mode_basis.reshape(nb, bs, m)
    index = stiffness_index.T
    owners = pair_owner.T
    lists = margin.transpose(1, 2, 3, 0)
    groups = 2
    hbm = lambda x: pltpu.with_memory_space_constraint(x, pltpu.HBM)
    total, modes_near, send_col, send_row = pl.pallas_call(
        functools.partial(apply_kernel, nk, cols, groups),
        out_shape=(
            pltpu.VMEM((nb, bs, m), F32),
            pltpu.VMEM((nb, bs, m), BF16),
            pltpu.VMEM((ovb, bs, m), BF16),
            pltpu.VMEM((ovb, bs, m), BF16),
        ),
        in_specs=[HBM] * 5,
        out_specs=(VMEM,) * 4,
        scratch_shapes=[
            pltpu.SMEM(index.shape, jnp.int32),
            pltpu.SMEM(owners.shape, jnp.int32),
            pltpu.SMEM(lists.shape, jnp.int32),
            pltpu.VMEM((nk, bs, bs), BF16),
            pltpu.SemaphoreType.DMA((3,)),
            pltpu.SemaphoreType.DMA,
            pltpu.SemaphoreType.DMA((groups,)),
        ],
        compiler_params=params(20),
        cost_estimate=pl.CostEstimate(
            flops=2 * nk * bs * bs * m, bytes_accessed=2 * (stiffness.size + 2 * mode_basis.size), transcendentals=0
        ),
        name="apply",
    )(hbm(index), hbm(owners), hbm(lists), hbm(stiffness), hbm(modes))

    got_row = lax.ppermute(send_row, "row", [(r, r - 1) for r in range(1, rows)])
    flat = rows * cols
    line = [(d, d - 1) for d in range(flat) if (d // cols) % 2 == 0 and d % cols > 0]
    line += [(d, d + 1) for d in range(flat) if (d // cols) % 2 == 1 and d % cols < cols - 1]
    got_col = lax.ppermute(send_col, ("row", "col"), line)

    part = m // cols
    stored, diag, keep_col, keep_row = pl.pallas_call(
        functools.partial(middle_kernel, cols),
        out_shape=(
            pltpu.HBM((cols, flat, part, m), BF16),
            pltpu.VMEM((m, m), BF16),
            pltpu.VMEM((m, ovb * bs), BF16),
            pltpu.VMEM((m, ovb * bs), BF16),
        ),
        in_specs=[HBM, HBM, VMEM, VMEM],
        out_specs=(HBM, VMEM, VMEM, VMEM),
        scratch_shapes=[
            pltpu.SMEM(owners.shape, jnp.int32),
            pltpu.SMEM(lists.shape, jnp.int32),
            pltpu.VMEM((flat, part, m), BF16),
            pltpu.VMEM((m, m), F32),
            pltpu.SemaphoreType.DMA((2,)),
            pltpu.SemaphoreType.DMA((cols,)),
        ],
        compiler_params=params(12),
        cost_estimate=pl.CostEstimate(
            flops=2 * mode_basis.size * m, bytes_accessed=2 * cols * flat * part * m, transcendentals=0
        ),
        name="middle",
    )(hbm(owners), hbm(lists), modes_near, total)

    order = exchange_order(cols)
    pieces = pl.pallas_call(
        functools.partial(project_kernel, order),
        out_shape=pltpu.VMEM((cols, 3 * part, m), BF16),
        in_specs=[VMEM] * 5,
        out_specs=VMEM,
        compiler_params=params(12),
        cost_estimate=pl.CostEstimate(
            flops=4 * ovb * bs * m * m, bytes_accessed=8 * ovb * bs * m, transcendentals=0
        ),
        name="project",
    )(diag, keep_col, keep_row, got_col.reshape(ovb * bs, m), got_row.reshape(ovb * bs, m))

    received = lax.all_to_all(
        pieces, "col", split_axis=0, concat_axis=0, axis_index_groups=[order], tiled=True
    )

    return pl.pallas_call(
        functools.partial(store_kernel, rows, order),
        out_shape=pltpu.HBM(stored.shape, BF16),
        in_specs=[VMEM, HBM],
        out_specs=HBM,
        scratch_shapes=[pltpu.SemaphoreType.DMA((3, cols))],
        input_output_aliases={1: 0},
        compiler_params=params(12),
        name="store",
    )(received, stored)


def solution(mesh):
    return jax.shard_map(
        on_device,
        mesh=mesh,
        in_specs=(
            P(("row", "col"), None, None),
            P(("row", "col"), None),
            P(("row", "col"), None),
            P(),
            P(),
        ),
        out_specs=P("row", None, "col", None),
        check_vma=False,
    )
```

```python
import functools

import jax
import jax.numpy as jnp
from jax import lax
from jax.experimental import pallas as pl
from jax.experimental.pallas import tpu as pltpu
from jax.sharding import PartitionSpec as P

F32 = jnp.float32
BF16 = jnp.bfloat16
HBM = pl.BlockSpec(memory_space=pltpu.HBM)
VMEM = pl.BlockSpec(memory_space=pltpu.VMEM)


def place():
    row = lax.axis_index("row")
    col = lax.axis_index("col")
    sub = row * lax.axis_size("col") + col
    return row, col, sub, lax.rem(row, 2)


def exchange_orders(cols):
    side = int(cols**0.5)
    y0, z0 = side // 2, side // 2
    steps = [(i, j) for i in range(side) for j in range(side)]
    even = [(y0 + i + j) % side * side + (z0 + j) % side for i, j in steps]
    odd = [(y0 + i) % side * side + (z0 + i + j) % side for i, j in steps]
    return even, odd


def side_block(owners, lists, direction, first, side, j):
    use_applied = owners[direction, first] + side == 1
    return lists[direction, j, side, first], use_applied


def sides(sub, odd, cols):
    before = jnp.maximum(sub - 1, 0)
    above = jnp.maximum(sub - cols, 0)
    send_col = (0, jnp.where(odd == 1, sub, before), 1 - odd)
    send_row = (1, above, 1)
    keep_col = (0, jnp.where(odd == 1, before, sub), odd)
    keep_row = (1, sub, 0)
    return send_col, send_row, keep_col, keep_row


def apply_kernel(
    nk, cols, index_hbm, owner_hbm, margin_hbm, stiff_hbm, modes_hbm,
    total, modes, send_col_ref, send_row_ref,
    index, owners, lists, stiff, small_sem, mode_sem, stiff_sem,
):
    small = [
        pltpu.make_async_copy(src, dst, small_sem.at[i])
        for i, (src, dst) in enumerate(((index_hbm, index), (owner_hbm, owners), (margin_hbm, lists)))
    ]
    mode_copy = pltpu.make_async_copy(modes_hbm, modes, mode_sem)
    edges = [0, nk * 3 // 7, nk]
    stiff_copies = [
        pltpu.make_async_copy(
            stiff_hbm.at[pl.ds(lo, hi - lo)], stiff.at[pl.ds(lo, hi - lo)], stiff_sem.at[g]
        )
        for g, (lo, hi) in enumerate(zip(edges, edges[1:]))
    ]
    small[0].start()
    mode_copy.start()
    for copy in stiff_copies:
        copy.start()
    small[1].start()
    small[2].start()
    total[...] = jnp.zeros_like(total)
    for copy in small:
        copy.wait()
    mode_copy.wait()
    for g in range(len(stiff_copies)):
        stiff_copies[g].wait()
        for k in range(edges[g], edges[g + 1]):
            product = jnp.dot(stiff[k], modes[index[1, k]], preferred_element_type=F32)
            a = index[0, k]
            total[a] = total[a] + product
    _, _, sub, odd = place()
    send_col, send_row, _, _ = sides(sub, odd, cols)
    for out, (direction, first, side) in ((send_row_ref, send_row), (send_col_ref, send_col)):
        for j in range(out.shape[0]):
            block, use_applied = side_block(owners, lists, direction, first, side, j)

            @pl.when(use_applied)
            def _():
                out[j] = total[block].astype(BF16)

            @pl.when(jnp.logical_not(use_applied))
            def _():
                out[j] = modes[block]


def middle_kernel(
    cols, owner_hbm, margin_hbm, modes, applied, stored, diag_ref, keep_col_ref, keep_row_ref,
    owners, lists, zeros, total, small_sem, zero_sem,
):
    small = [
        pltpu.make_async_copy(src, dst, small_sem.at[i])
        for i, (src, dst) in enumerate(((owner_hbm, owners), (margin_hbm, lists)))
    ]
    for copy in small:
        copy.start()
    zeros[...] = jnp.zeros_like(zeros)
    fills = [
        pltpu.make_async_copy(zeros, stored.at[i], zero_sem.at[i]) for i in range(stored.shape[0])
    ]
    for fill in fills:
        fill.start()
    total[...] = jnp.zeros_like(total)

    def step(a, carry):
        total[...] += lax.dot_general(
            modes[a], applied[a].astype(BF16), (((0,), (0,)), ((), ())), preferred_element_type=F32
        )
        return carry

    lax.fori_loop(0, modes.shape[0], step, 0)
    diag_ref[...] = total[...].astype(BF16)
    for copy in small:
        copy.wait()
    _, _, sub, odd = place()
    _, _, keep_col, keep_row = sides(sub, odd, cols)
    bs = modes.shape[1]
    for out, (direction, first, side) in ((keep_col_ref, keep_col), (keep_row_ref, keep_row)):
        for j in range(out.shape[1] // bs):
            block, use_applied = side_block(owners, lists, direction, first, side, j)

            @pl.when(use_applied)
            def _():
                out[:, j * bs : (j + 1) * bs] = applied[block].astype(BF16).T

            @pl.when(jnp.logical_not(use_applied))
            def _():
                out[:, j * bs : (j + 1) * bs] = modes[block].T

    for fill in fills:
        fill.wait()


def project_kernel(orders, diag, keep_col, keep_row, got_col, got_row, pieces):
    part = pieces.shape[1] // 3
    row_block = jnp.dot(keep_row[...], got_row[...], preferred_element_type=F32).astype(BF16)
    col_block = jnp.dot(keep_col[...], got_col[...], preferred_element_type=F32)
    odd = lax.rem(lax.axis_index("row"), 2)

    def spread(order, column):
        for p, c in enumerate(order):
            pieces[p, 0:part] = diag[c * part : (c + 1) * part]
            pieces[p, part : 2 * part] = column[c * part : (c + 1) * part]
            pieces[p, 2 * part : 3 * part] = row_block[c * part : (c + 1) * part]

    @pl.when(odd == 0)
    def _():
        spread(orders[0], col_block.astype(BF16))

    @pl.when(odd == 1)
    def _():
        spread(orders[1], col_block.T.astype(BF16))


def store_kernel(rows, orders, received, zeroed, stored, sems):
    del zeroed
    cols = received.shape[0]
    part = received.shape[1] // 3
    row = lax.axis_index("row")
    odd = lax.rem(row, 2)
    base = row * cols

    def copies(act, parity, order):
        for p, c in enumerate(order):
            act(pltpu.make_async_copy(received.at[p, 0:part], stored.at[c, base + c], sems.at[0, p]))
            first = c - parity
            if 0 <= first < cols - 1:
                act(
                    pltpu.make_async_copy(
                        received.at[p, part : 2 * part], stored.at[first, base + first + 1], sems.at[1, p]
                    )
                )

        @pl.when(row < rows - 1)
        def _():
            for p, c in enumerate(order):
                act(
                    pltpu.make_async_copy(
                        received.at[p, 2 * part : 3 * part], stored.at[c, base + cols + c], sems.at[2, p]
                    )
                )

    for parity, order in enumerate(orders):

        @pl.when(odd == parity)
        def _():
            copies(lambda copy: copy.start(), parity, order)
            copies(lambda copy: copy.wait(), parity, order)


def params(mib):
    return pltpu.CompilerParams(vmem_limit_bytes=mib << 20)


def on_device(stiffness, stiffness_index, mode_basis, pair_owner, margin):
    rows = lax.axis_size("row")
    cols = lax.axis_size("col")
    nk, bs, _ = stiffness.shape
    m = mode_basis.shape[1]
    nb = mode_basis.shape[0] // bs
    ovb = margin.shape[2]
    modes = mode_basis.reshape(nb, bs, m)
    index = stiffness_index.T
    owners = pair_owner.T
    lists = margin.transpose(1, 2, 3, 0)
    hbm = lambda x: pltpu.with_memory_space_constraint(x, pltpu.HBM)
    total, modes_near, send_col, send_row = pl.pallas_call(
        functools.partial(apply_kernel, nk, cols),
        out_shape=(
            pltpu.VMEM((nb, bs, m), F32),
            pltpu.VMEM((nb, bs, m), BF16),
            pltpu.VMEM((ovb, bs, m), BF16),
            pltpu.VMEM((ovb, bs, m), BF16),
        ),
        in_specs=[HBM] * 5,
        out_specs=(VMEM,) * 4,
        scratch_shapes=[
            pltpu.SMEM(index.shape, jnp.int32),
            pltpu.SMEM(owners.shape, jnp.int32),
            pltpu.SMEM(lists.shape, jnp.int32),
            pltpu.VMEM((nk, bs, bs), BF16),
            pltpu.SemaphoreType.DMA((3,)),
            pltpu.SemaphoreType.DMA,
            pltpu.SemaphoreType.DMA((2,)),
        ],
        compiler_params=params(20),
        cost_estimate=pl.CostEstimate(
            flops=2 * nk * bs * bs * m, bytes_accessed=2 * (stiffness.size + 2 * mode_basis.size), transcendentals=0
        ),
        name="apply",
    )(hbm(index), hbm(owners), hbm(lists), hbm(stiffness), hbm(modes))

    got_row = lax.ppermute(send_row, "row", [(r, r - 1) for r in range(1, rows)])
    flat = rows * cols
    line = [(d, d - 1) for d in range(flat) if (d // cols) % 2 == 0 and d % cols > 0]
    line += [(d, d + 1) for d in range(flat) if (d // cols) % 2 == 1 and d % cols < cols - 1]
    got_col = lax.ppermute(send_col, ("row", "col"), line)

    part = m // cols
    stored, diag, keep_col, keep_row = pl.pallas_call(
        functools.partial(middle_kernel, cols),
        out_shape=(
            pltpu.HBM((cols, flat, part, m), BF16),
            pltpu.VMEM((m, m), BF16),
            pltpu.VMEM((m, ovb * bs), BF16),
            pltpu.VMEM((m, ovb * bs), BF16),
        ),
        in_specs=[HBM, HBM, VMEM, VMEM],
        out_specs=(HBM, VMEM, VMEM, VMEM),
        scratch_shapes=[
            pltpu.SMEM(owners.shape, jnp.int32),
            pltpu.SMEM(lists.shape, jnp.int32),
            pltpu.VMEM((flat, part, m), BF16),
            pltpu.VMEM((m, m), F32),
            pltpu.SemaphoreType.DMA((2,)),
            pltpu.SemaphoreType.DMA((cols,)),
        ],
        compiler_params=params(12),
        cost_estimate=pl.CostEstimate(
            flops=2 * mode_basis.size * m, bytes_accessed=2 * cols * flat * part * m, transcendentals=0
        ),
        name="middle",
    )(hbm(owners), hbm(lists), modes_near, total)

    orders = exchange_orders(cols)
    pieces = pl.pallas_call(
        functools.partial(project_kernel, orders),
        out_shape=pltpu.VMEM((cols, 3 * part, m), BF16),
        in_specs=[VMEM] * 5,
        out_specs=VMEM,
        compiler_params=params(12),
        cost_estimate=pl.CostEstimate(
            flops=4 * ovb * bs * m * m, bytes_accessed=8 * ovb * bs * m, transcendentals=0
        ),
        name="project",
    )(diag, keep_col, keep_row, got_col.reshape(ovb * bs, m), got_row.reshape(ovb * bs, m))

    received = lax.all_to_all(
        pieces,
        ("row", "col"),
        split_axis=0,
        concat_axis=0,
        axis_index_groups=[[r * cols + c for c in orders[r % 2]] for r in range(rows)],
        tiled=True,
    )

    return pl.pallas_call(
        functools.partial(store_kernel, rows, orders),
        out_shape=pltpu.HBM(stored.shape, BF16),
        in_specs=[VMEM, HBM],
        out_specs=HBM,
        scratch_shapes=[pltpu.SemaphoreType.DMA((3, cols))],
        input_output_aliases={1: 0},
        compiler_params=params(12),
        name="store",
    )(received, stored)


def solution(mesh):
    return jax.shard_map(
        on_device,
        mesh=mesh,
        in_specs=(
            P(("row", "col"), None, None),
            P(("row", "col"), None),
            P(("row", "col"), None),
            P(),
            P(),
        ),
        out_specs=P("row", None, "col", None),
        check_vma=False,
    )
```
